256 devices in a mesh: fsdp: 32 (over y_hi, z, core), grp: 8 (over y_lo, x).
Axes of the slice: x: 4, y: 4 (y_hi: 2, y_lo: 2; y = y_hi * 2 + y_lo), z: 8, core: 2. Of those that a mesh axis runs over, the one named last changes fastest.
Arguments:
- hidden_act: bfloat16 [8, 2048, 14336], P('grp', None, 'fsdp'), may hold values from -6 to 6
- grad_output: bfloat16 [8, 2048, 4096], P('grp', 'fsdp'), may hold values from -6 to 6
- down_weight: bfloat16 [14336, 4096], P('fsdp'), may hold values from -0.09375 to 0.09375
- proj_in: bfloat16 [14336, 64], P('fsdp'), may hold values from -0.046875 to 0.046875
- proj_out: bfloat16 [4096, 64], replicated, may hold values from -0.09375 to 0.09375
- example_ids: int32 [8, 2048], P('grp'), may hold values from 0 to 7, never falling along the last dimension, each value on 1 to 512 neighbouring positions
Outputs:
- grad_hidden: bfloat16 [8, 2048, 14336], P('grp', None, 'fsdp')
- gram: float32 [4096, 4096], P('grp', 'fsdp')
- scores: float32 [64], replicated
The draws below stay inside these ranges and needn't reach their ends.
Inputs may be any that keep to these rules, and one draw needn't show every extreme that they name: `example_ids`: never falls along a group's tokens; each of the 8 examples of a group has 1 to 512 tokens, one exactly 512.
All inputs are finite; a program needn't handle non-finite values.
Results may differ from the reference program's by a relative error of at most 0.001.
Values may be sent and summed in bfloat16 or wider, within the bound.
No kernel may reach another device: no remote copies, remote signals or barrier semaphores. Data moves between devices by JAX's collectives and lax.ppermute only.
A program may use at most 128 MiB of HBM per device.

```python
import math
import jax
import jax.numpy as jnp
import numpy as np
from jax import lax

D = 4096
FF = 14336
PROJ = 64
TOK_GRP = 2048
EX_GRP = 8
EX_MOST = 512
GROUPS = 8


def block_levels(key, shape, pieces, low, high):
    level, own = 1.0, jax.random.fold_in(key, 6)
    for position, shards_of in pieces:
        steps = jnp.exp(jax.random.uniform(jax.random.fold_in(own, position), (shards_of,), jnp.float32, low / len(pieces), high / len(pieces)))
        level = level * jnp.repeat(steps, shape[position] // shards_of).reshape([-1 if axis == position else 1 for axis in range(len(shape))])
    return level


def split_up(number_of, total, bound, slope):
    portions = [(1 << 20) // math.isqrt(rank ** slope) + 1 for rank in range(2, number_of + 1)]
    spare, holding = total - bound - (number_of - 1), [1] * (number_of - 1)
    while spare > 0:
        movable = [i for i in range(number_of - 1) if holding[i] < bound]
        pool, budget = sum([portions[i] for i in movable]), spare
        for i in movable:
            addition = min(bound - holding[i], max(1, budget * portions[i] // pool), spare)
            holding[i] = holding[i] + addition
            spare = spare - addition
    return np.array([bound] + holding)


def ragged(rng, number_of, total, most, slope):
    if number_of == 2:
        one = jax.random.randint(rng, (), max(1, total - most), min(most, total - 1) + 1)
        return jnp.stack([one, total - one])
    tallies = jnp.asarray(split_up(number_of, total, most, slope), jnp.int32)
    couples = (number_of - 1) // 2
    donor, receiver = tallies[1:1 + 2 * couples:2], tallies[2:2 + 2 * couples:2]
    margin = jnp.minimum(donor - 1, most - receiver)
    moved = jax.random.randint(jax.random.fold_in(rng, 1), (couples,), 0, 1 << 20) % (margin + 1)
    tallies = tallies.at[1:1 + 2 * couples:2].set(donor - moved).at[2:2 + 2 * couples:2].set(receiver + moved)
    return tallies[jax.random.permutation(jax.random.fold_in(rng, 2), number_of)]


def normal_values(stream_key, shape, scale, limit, pieces=(), held_as=jnp.bfloat16):
    level = block_levels(stream_key, shape, pieces, -0.22, 0.18) if pieces else 1.0
    result = jax.random.normal(stream_key, shape, jnp.float32) * scale * level
    return jnp.minimum(jnp.maximum(result, -limit), limit).astype(held_as)


def setup_inputs(seed: int = 0) -> dict:
    streams_of = jax.random.split(jax.random.key(seed), 7)
    hidden_act = normal_values(streams_of[0], (GROUPS, TOK_GRP, FF), 1.0, 6.0, ((0, 8), (2, 32)))
    grad_output = normal_values(streams_of[1], (GROUPS, TOK_GRP, D), 1.0, 6.0, ((0, 8), (1, 32)))
    down_weight = normal_values(streams_of[2], (FF, D), D ** -0.5, 0.09375, ((0, 32),))
    proj_in = normal_values(streams_of[3], (FF, PROJ), FF ** -0.5, 0.046875, ((0, 32),))
    proj_out = normal_values(streams_of[4], (D, PROJ), D ** -0.5, 0.09375)
    example_ids = jax.vmap(lambda own: jnp.searchsorted(jnp.cumsum(ragged(own, EX_GRP, TOK_GRP, EX_MOST, 2)), jnp.arange(TOK_GRP), side="right"))(jax.random.split(streams_of[5], GROUPS)).reshape((GROUPS, TOK_GRP)).astype(jnp.int32)
    return {"hidden_act": hidden_act, "grad_output": grad_output, "down_weight": down_weight, "proj_in": proj_in, "proj_out": proj_out, "example_ids": example_ids}


def inverse_diagonal(matrix):
    lower = jnp.linalg.cholesky(matrix)
    eye = jnp.eye(matrix.shape[0], dtype=matrix.dtype)
    lower_inv = jax.scipy.linalg.solve_triangular(lower, eye, lower=True)
    return jnp.sum(lower_inv * lower_inv, axis=0)

def reference(hidden_act, grad_output, down_weight, proj_in, proj_out, example_ids):
    groups = hidden_act.shape[0]
    flat_h = hidden_act.reshape(-1, FF)
    flat_g = grad_output.reshape(-1, D)
    grad_hidden = lax.dot_general(flat_g.astype(jnp.float32), down_weight.astype(jnp.float32), (((1,), (1,)), ((), ())), preferred_element_type=jnp.float32)
    grad_hidden = grad_hidden.astype(jnp.bfloat16).reshape(hidden_act.shape)
    left = jnp.dot(flat_h.astype(jnp.float32), proj_in.astype(jnp.float32), preferred_element_type=jnp.float32).reshape(groups, TOK_GRP, PROJ)
    right = jnp.dot(flat_g.astype(jnp.float32), proj_out.astype(jnp.float32), preferred_element_type=jnp.float32).reshape(groups, TOK_GRP, PROJ)
    onehot = (example_ids[:, None, :] == jnp.arange(EX_GRP, dtype=jnp.int32)[None, :, None]).astype(jnp.float32)
    feats = jnp.einsum('get,gti,gtj->geij', onehot, left, right, precision=lax.Precision.HIGHEST)
    feats = feats.reshape(groups * EX_GRP, PROJ * PROJ) * (EX_GRP / TOK_GRP) ** 0.5
    examples = groups * EX_GRP
    gram = jnp.dot(feats.T, feats, precision=lax.Precision.HIGHEST) / examples
    kernel = jnp.dot(feats, feats.T, precision=lax.Precision.HIGHEST)
    ridge = jnp.trace(kernel) / examples
    eye = jnp.eye(examples, dtype=kernel.dtype)
    scores = 1.0 - ridge * inverse_diagonal(kernel + ridge * eye)
    return (grad_hidden, gram, scores)
```

```python
import functools

import jax
import jax.numpy as jnp
from jax import lax
from jax.experimental import pallas as pl
from jax.experimental.pallas import tpu as pltpu
from jax.sharding import PartitionSpec as P

PROJ = 64
TOK_GRP = 2048
EX_GRP = 8
LANES = 128
PLANES = 2
RING = 8
CORES = 2
CHIPS = PLANES * RING
SAME_CORE = [[chip * CORES + core for chip in range(CHIPS)] for core in range(CORES)]
NT = (((1,), (1,)), ((), ()))


def device_perm(move):
    pairs = []
    for plane in range(PLANES):
        for z in range(RING):
            for core in range(CORES):
                to_plane, to_z, to_core = move(plane, z, core)
                pairs.append(
                    (
                        (plane * RING + z) * CORES + core,
                        (to_plane * RING + to_z % RING) * CORES + to_core,
                    )
                )
    return pairs


UP = device_perm(lambda plane, z, core: (plane, z + 1, core))
DOWN = device_perm(lambda plane, z, core: (plane, z - 1, core))
ACROSS = device_perm(lambda plane, z, core: (1 - plane, z, core))
SWAP = device_perm(lambda plane, z, core: (plane, z, 1 - core))


def permute(value, pairs):
    return lax.ppermute(value, "fsdp", pairs)


def matmul_kernel(count, place_ref, *refs):
    weight_ref = refs[0]
    block_refs = refs[1 : 1 + 2 * count]
    out_ref, total, rows, rounded, sems = refs[-5:]
    step = pl.program_id(0)
    core = place_ref[count]
    for b in range(count):
        mine = pl.multiple_of(b * LANES + core * 64, 64)
        other = pl.multiple_of(b * LANES + (1 - core) * 64, 64)
        rows[pl.ds(mine, 64), :] = block_refs[2 * b][...]
        rows[pl.ds(other, 64), :] = block_refs[2 * b + 1][...]
    part = lax.dot_general(
        weight_ref[...], rows[...], NT, preferred_element_type=jnp.float32
    )

    @pl.when(step == 0)
    def _():
        total[...] = part

    @pl.when(step > 0)
    def _():
        total[...] += part

    @pl.when(step == pl.num_programs(0) - 1)
    def _():
        rounded[...] = total[...].astype(jnp.bfloat16)
        copies = []
        for b in range(count):
            column = pl.multiple_of(place_ref[b] * LANES, LANES)
            copies.append(
                pltpu.make_async_copy(
                    rounded.at[:, pl.ds(b * LANES, LANES)],
                    out_ref.at[:, pl.ds(column, LANES)],
                    sems.at[b],
                )
            )
        for copy in copies:
            copy.start()
        for copy in copies:
            copy.wait()


def matmul_blocks(weight, blocks, places, core, out, tokens):
    count = len(blocks)
    width, depth = weight.shape
    steps = 4
    chunk = depth // steps
    flat = [array for pair in blocks for array in pair]
    place = jnp.stack([*places, core]).astype(jnp.int32)
    in_specs = [pl.BlockSpec((width, chunk), lambda k, _: (0, k))]
    in_specs += [pl.BlockSpec((64, chunk), lambda k, _: (0, k))] * (2 * count)
    args = [place, weight, *flat]
    aliases = {}
    if out is not None:
        in_specs.append(pl.BlockSpec(memory_space=pl.ANY))
        args.append(out)
        aliases = {len(args) - 1: 0}
    return pl.pallas_call(
        functools.partial(matmul_kernel, count),
        out_shape=jax.ShapeDtypeStruct((width, tokens), jnp.bfloat16),
        grid_spec=pltpu.PrefetchScalarGridSpec(
            num_scalar_prefetch=1,
            grid=(steps,),
            in_specs=in_specs,
            out_specs=pl.BlockSpec(memory_space=pl.ANY),
            scratch_shapes=[
                pltpu.VMEM((width, count * LANES), jnp.float32),
                pltpu.VMEM((count * LANES, chunk), jnp.bfloat16),
                pltpu.VMEM((width, count * LANES), jnp.bfloat16),
                pltpu.SemaphoreType.DMA((count,)),
            ],
        ),
        input_output_aliases=aliases,
        compiler_params=pltpu.CompilerParams(
            dimension_semantics=("arbitrary",), vmem_limit_bytes=40 << 20
        ),
    )(*args)


def inverse_diagonal(matrix):
    lower = jnp.linalg.cholesky(matrix)
    eye = jnp.eye(matrix.shape[0], dtype=matrix.dtype)
    lower_inv = jax.scipy.linalg.solve_triangular(lower, eye, lower=True)
    return jnp.sum(lower_inv * lower_inv, axis=0)


def body(hidden_act, grad_output, down_weight, proj_in, proj_out, example_ids):
    group_count = lax.axis_size("grp")
    examples = EX_GRP * group_count
    device = lax.axis_index("fsdp")
    core = device % CORES
    plane = device // (RING * CORES)
    z = (device // CORES) % RING
    hidden = hidden_act[0]
    grad_rows = grad_output[0]
    ids = example_ids[0]

    own = {0: grad_rows}
    far = {}
    own[-1] = permute(own[0], UP)
    own[1] = permute(own[0], DOWN)
    far[0] = permute(own[0], ACROSS)
    own[-2] = permute(own[-1], UP)
    own[2] = permute(own[1], DOWN)
    far[1] = permute(own[1], ACROSS)
    own[-3] = permute(own[-2], UP)
    own[3] = permute(own[2], DOWN)
    far[-1] = permute(own[-1], ACROSS)
    far[-2] = permute(far[-1], UP)
    own[4] = permute(own[3], DOWN)
    far[2] = permute(own[2], ACROSS)
    far[-3] = permute(far[-2], UP)
    far[3] = permute(far[2], DOWN)
    far[4] = permute(own[4], ACROSS)

    pair_rows = permute(grad_rows, SWAP)

    def block(table, offset, other):
        side = plane if table is own else 1 - plane
        if table is own and offset == 0:
            second = pair_rows
        else:
            second = permute(table[offset], SWAP)
        return (table[offset], second), side * RING + (z + offset) % RING

    out = None
    slots = [
        [(own, 0)],
        [(own, -1), (own, 1), (far, 0)],
        [(own, -2), (own, 2), (far, 1)],
        [(own, -3), (own, 3), (far, -1)],
        [(far, -2), (own, 4), (far, 2)],
        [(far, -3), (far, 3), (far, 4)],
    ]
    for slot in slots:
        made = [block(table, offset, None) for table, offset in slot]
        out = matmul_blocks(
            down_weight, [m[0] for m in made], [m[1] for m in made], core, out, TOK_GRP
        )
    grad_hidden = jnp.transpose(out)[None]

    half = PROJ // CORES
    left = lax.dot_general(
        proj_in, hidden, (((0,), (1,)), ((), ())), preferred_element_type=jnp.float32
    )
    kept = lax.dynamic_slice_in_dim(left, core * half, half, 0)
    given = lax.dynamic_slice_in_dim(left, (1 - core) * half, half, 0)
    kept = kept + permute(given, SWAP)
    right_rows = lax.dynamic_slice_in_dim(jnp.transpose(proj_out), core * half, half, 0)
    mine = lax.dot_general(right_rows, grad_rows, NT, preferred_element_type=jnp.float32)
    other = lax.dot_general(right_rows, pair_rows, NT, preferred_element_type=jnp.float32)
    right = jnp.where(
        core == 0,
        jnp.concatenate([mine, other], axis=1),
        jnp.concatenate([other, mine], axis=1),
    )
    packed = jnp.concatenate(
        [
            kept.reshape(CHIPS, 2 * TOK_GRP // LANES, LANES),
            jnp.broadcast_to(right[None], (CHIPS, half, LANES)),
        ],
        axis=1,
    )
    packed = lax.all_to_all(
        packed, "fsdp", 0, 0, axis_index_groups=SAME_CORE, tiled=True
    )
    left_two = jnp.sum(packed[:, :half], axis=0).reshape(2, TOK_GRP)
    right_all = jnp.transpose(packed[:, half:], (1, 0, 2)).reshape(half, TOK_GRP)
    left_other = permute(left_two, SWAP)
    left_four = jnp.where(
        core == 0,
        jnp.concatenate([left_two, left_other], axis=0),
        jnp.concatenate([left_other, left_two], axis=0),
    )
    onehot = (jnp.arange(EX_GRP, dtype=jnp.int32)[:, None] == ids[None, :]).astype(
        jnp.float32
    )
    weighted = (onehot[:, None, :] * left_four[None]).reshape(EX_GRP * 4, TOK_GRP)
    feats = lax.dot_general(weighted, right_all, NT, precision=lax.Precision.HIGHEST)
    feats = feats.reshape(EX_GRP, 4 * half) * (EX_GRP / TOK_GRP) ** 0.5
    feats = lax.all_to_all(
        jnp.broadcast_to(feats[None], (CHIPS, EX_GRP, LANES)),
        "fsdp",
        0,
        0,
        axis_index_groups=SAME_CORE,
        tiled=True,
    )
    feats = lax.all_to_all(
        jnp.broadcast_to(
            feats.reshape(1, CHIPS * EX_GRP, LANES),
            (group_count, CHIPS * EX_GRP, LANES),
        ),
        "grp",
        0,
        0,
        tiled=True,
    )
    feats_other = permute(feats, SWAP)
    low = jnp.where(core == 0, feats, feats_other)
    high = jnp.where(core == 0, feats_other, feats)

    def spread(part):
        part = part.reshape(group_count, CHIPS, EX_GRP, 2, 2, half)
        part = jnp.transpose(part, (0, 2, 3, 1, 4, 5))
        return part.reshape(examples, PROJ, half)

    full = jnp.concatenate([spread(low), spread(high)], axis=2).reshape(
        examples, PROJ * PROJ
    )
    row_count = PROJ * PROJ // group_count
    col_count = PROJ * PROJ // (CHIPS * CORES)
    own_rows = lax.dynamic_slice_in_dim(
        full, lax.axis_index("grp") * row_count, row_count, 1
    )
    own_cols = lax.dynamic_slice_in_dim(full, device * col_count, col_count, 1)
    gram = (
        lax.dot_general(
            own_rows,
            own_cols,
            (((0,), (0,)), ((), ())),
            precision=lax.Precision.HIGHEST,
            preferred_element_type=jnp.float32,
        )
        / examples
    )
    kernel = lax.dot_general(
        full,
        full,
        NT,
        precision=lax.Precision.HIGHEST,
        preferred_element_type=jnp.float32,
    )
    ridge = jnp.trace(kernel) / examples
    eye = jnp.eye(examples, dtype=jnp.float32)
    scores = 1.0 - ridge * inverse_diagonal(kernel + ridge * eye)
    return (grad_hidden, gram, scores)


def solution(mesh):
    in_specs = (
        P("grp", None, "fsdp"),
        P("grp", "fsdp", None),
        P("fsdp", None),
        P("fsdp", None),
        P(),
        P("grp", None),
    )
    out_specs = (P("grp", None, "fsdp"), P("grp", "fsdp"), P())
    return jax.shard_map(body, mesh=mesh, in_specs=in_specs, out_specs=out_specs, check_vma=False)
```

```python
import functools

import jax
import jax.numpy as jnp
from jax import lax
from jax.experimental import pallas as pl
from jax.experimental.pallas import tpu as pltpu
from jax.sharding import PartitionSpec as P

PROJ = 64
TOK_GRP = 2048
EX_GRP = 8
LANES = 128
PLANES = 2
RING = 8
CORES = 2
CHIPS = PLANES * RING
SAME_CORE = [[chip * CORES + core for chip in range(CHIPS)] for core in range(CORES)]
HALF = PROJ // CORES
NT = (((1,), (1,)), ((), ()))
TN = (((0,), (0,)), ((), ()))
NN = (((1,), (0,)), ((), ()))
EXACT = lax.Precision.HIGHEST
VMEM = pl.BlockSpec(memory_space=pltpu.VMEM)
SMEM = pl.BlockSpec(memory_space=pltpu.SMEM)
ANY = pl.BlockSpec(memory_space=pltpu.HBM)


def device_perm(move):
    pairs = []
    for plane in range(PLANES):
        for z in range(RING):
            for core in range(CORES):
                to_plane, to_z, to_core = move(plane, z, core)
                pairs.append(
                    (
                        (plane * RING + z) * CORES + core,
                        (to_plane * RING + to_z % RING) * CORES + to_core,
                    )
                )
    return pairs


UP = device_perm(lambda plane, z, core: (plane, z + 1, core))
DOWN = device_perm(lambda plane, z, core: (plane, z - 1, core))
ACROSS = device_perm(lambda plane, z, core: (1 - plane, z, core))
SWAP = device_perm(lambda plane, z, core: (plane, z, 1 - core))


def permute(value, pairs):
    return lax.ppermute(value, "fsdp", pairs)


def call(
    kernel, name, room, out_shape, args, scratch=(), in_specs=None, out_specs=None, aliases=None
):
    return pl.pallas_call(
        kernel,
        name=name,
        out_shape=out_shape,
        in_specs=in_specs or [SMEM] + [VMEM] * (len(args) - 1),
        out_specs=out_specs
        or (VMEM if not isinstance(out_shape, tuple) else (VMEM,) * len(out_shape)),
        scratch_shapes=list(scratch),
        input_output_aliases=aliases or {},
        compiler_params=pltpu.CompilerParams(vmem_limit_bytes=room << 20),
        cost_estimate=pl.CostEstimate(flops=0, transcendentals=0, bytes_accessed=0),
    )(*args)


def in_hbm(value):
    return pltpu.with_memory_space_constraint(value, pltpu.HBM)


def f32(*shape):
    return jax.ShapeDtypeStruct(shape, jnp.float32)


def matmul_kernel(count, place_ref, weight_hbm, *refs):
    block_refs = refs[: 2 * count]
    out_ref, weight, rows, rounded, weight_sems, row_sems, out_sems = refs[-7:]
    core = place_ref[count]
    wide = 2 * LANES
    height = weight_hbm.shape[0] // 2
    weights = [
        pltpu.make_async_copy(
            weight_hbm.at[pl.ds(i * height, height)],
            weight.at[pl.ds(i * height, height)],
            weight_sems.at[i],
        )
        for i in range(2)
    ]
    for load in weights:
        load.start()
    for b in range(count):
        for side, half in enumerate((core, 1 - core)):
            start = pl.multiple_of(b * LANES + half * 64, 64)
            pltpu.make_async_copy(
                block_refs[2 * b + side], rows.at[pl.ds(start, 64)], row_sems.at[2 * b + side]
            ).start()
    for load in weights:
        load.wait()

    def store(i, b):
        column = pl.multiple_of(place_ref[2 * i + b] * LANES, LANES)
        return pltpu.make_async_copy(
            rounded.at[i, :, pl.ds(b * LANES, LANES)],
            out_ref.at[:, pl.ds(column, LANES)],
            out_sems.at[2 * i + b],
        )

    def pair(i, carry):
        start = pl.multiple_of(i * wide, wide)
        for quarter in range(4):
            pltpu.make_async_copy(
                block_refs[0], rows.at[pl.ds(start + quarter * 64, 64)], row_sems.at[4 * i + quarter]
            ).wait()
        rounded[i] = lax.dot_general(
            weight[...], rows[pl.ds(start, wide), :], NT, preferred_element_type=jnp.float32
        ).astype(jnp.bfloat16)
        for b in range(2):
            store(i, b).start()
        return carry

    lax.fori_loop(0, count // 2, pair, 0)
    for b in range(count):
        store(b // 2, b % 2).wait()


def matmul_blocks(weight, blocks, places, core, out, tokens):
    count = len(blocks)
    width, depth = weight.shape
    flat = [array for pair in blocks for array in pair]
    args = [jnp.stack([*places, core]).astype(jnp.int32), *map(in_hbm, [weight, *flat])]
    aliases = {}
    if out is not None:
        args.append(out)
        aliases = {len(args) - 1: 0}
    return call(
        functools.partial(matmul_kernel, count),
        "grad_columns",
        14,
        jax.ShapeDtypeStruct((width, tokens), jnp.bfloat16),
        args,
        [
            pltpu.VMEM((width, depth), jnp.bfloat16),
            pltpu.VMEM((count * LANES, depth), jnp.bfloat16),
            pltpu.VMEM((count // 2, width, 2 * LANES), jnp.bfloat16),
            pltpu.SemaphoreType.DMA((2,)),
            pltpu.SemaphoreType.DMA((2 * count,)),
            pltpu.SemaphoreType.DMA((count,)),
        ],
        [SMEM] + [ANY] * (len(args) - 1),
        ANY,
        aliases,
    )


def project_kernel(
    info_ref, hidden_hbm, proj_in_hbm, rows_hbm, proj_out_hbm, kept_ref, given_ref,
    hidden, proj_in, rows, proj_out, both, sems
):
    core = info_ref[0]
    parts = 4
    width = TOK_GRP // parts
    chunks = [
        pltpu.make_async_copy(
            hidden_hbm.at[:, pl.ds(i * width, width)],
            hidden.at[:, pl.ds(i * width, width)],
            sems.at[i],
        )
        for i in range(parts)
    ]
    small = [
        pltpu.make_async_copy(source, target, sems.at[parts + i])
        for i, (source, target) in enumerate(
            ((proj_in_hbm, proj_in), (rows_hbm, rows), (proj_out_hbm, proj_out))
        )
    ]
    for load in (small[0], *chunks, small[1], small[2]):
        load.start()
    small[0].wait()
    for i in range(parts):
        chunks[i].wait()
        lanes = slice(i * width, (i + 1) * width)
        both[:, lanes] = lax.dot_general(
            proj_in[...], hidden[:, lanes], NN, preferred_element_type=jnp.float32
        )
    small[1].wait()
    small[2].wait()
    right = lax.dot_general(proj_out[...], rows[...], NT, preferred_element_type=jnp.float32)
    both[:, TOK_GRP:] = jnp.concatenate([right, jnp.zeros_like(right)], axis=1)
    kept_ref[...] = both[pl.ds(pl.multiple_of(core * HALF, HALF), HALF), :]
    given_ref[...] = both[pl.ds(pl.multiple_of((1 - core) * HALF, HALF), HALF), :]


def pack_kernel(info_ref, kept_ref, taken_ref, out_ref):
    core = info_ref[0]
    for block in range(TOK_GRP // LANES):
        lanes = slice(block * LANES, (block + 1) * LANES)
        total = kept_ref[:, lanes] + taken_ref[:, lanes]
        out_ref[:, 2 * block : 2 * block + 2, :] = total.reshape(CHIPS, 2, LANES)
    kept = kept_ref[:, TOK_GRP : TOK_GRP + 64]
    taken = taken_ref[:, TOK_GRP : TOK_GRP + 64]
    right = jnp.where(
        core == 0,
        jnp.concatenate([kept, taken], axis=1),
        jnp.concatenate([taken, kept], axis=1),
    )
    out_ref[:, HALF:, :] = jnp.broadcast_to(right[None], (CHIPS, HALF, LANES))


def left_kernel(info_ref, packed_ref, out_ref):
    total = packed_ref[0, :HALF, :]
    for chip in range(1, CHIPS):
        total += packed_ref[chip, :HALF, :]
    out_ref[...] = total


def feats_kernel(info_ref, packed_ref, left_ref, other_ref, ids_ref, out_ref, weighted, right):
    core = info_ref[0]
    low = jnp.where(core == 0, left_ref[...], other_ref[...])
    high = jnp.where(core == 0, other_ref[...], left_ref[...])
    example = lax.broadcasted_iota(jnp.int32, (EX_GRP, LANES), 0)
    for block in range(TOK_GRP // LANES):
        lanes = slice(block * LANES, (block + 1) * LANES)
        mine = ids_ref[:, lanes] == example
        for column in range(4):
            source = low if column < 2 else high
            row = 2 * block + column % 2
            weighted[column * EX_GRP : (column + 1) * EX_GRP, lanes] = jnp.where(
                mine, source[row : row + 1, :], 0.0
            )
        right[:, lanes] = packed_ref[block, HALF:, :]
    sums = lax.dot_general(
        weighted[...], right[...], NT, precision=EXACT, preferred_element_type=jnp.float32
    )
    sums = sums * (EX_GRP / TOK_GRP) ** 0.5
    wide = jnp.concatenate(
        [sums[c * EX_GRP : (c + 1) * EX_GRP, :] for c in range(4)], axis=1
    )
    out_ref[...] = jnp.broadcast_to(wide[None], out_ref.shape)


def finish_kernel(examples, info_ref, mine_ref, other_ref, gram_ref, scores_ref, full):
    core, device, group = info_ref[0], info_ref[1], info_ref[2]
    for chip in range(CHIPS):
        rows = slice(chip * EX_GRP, (chip + 1) * EX_GRP)
        for part, ref in enumerate((mine_ref, other_ref)):
            start = (part * CHIPS + chip) * LANES
            full[:, start : start + LANES] = ref[:, rows, :].reshape(examples, LANES)

    def columns(chip, upper):
        start = pl.multiple_of(chip * EX_GRP, EX_GRP)
        halves = []
        for ref in (mine_ref, other_ref):
            part = ref[:, pl.ds(start, EX_GRP), :].reshape(examples, LANES)
            halves.append(jnp.where(upper == 0, part[:, :64], part[:, 64:]))
        first = jnp.where(core == 0, halves[0], halves[1])
        second = jnp.where(core == 0, halves[1], halves[0])
        return jnp.concatenate(
            [first[:, :HALF], second[:, :HALF], first[:, HALF:], second[:, HALF:]], axis=1
        )

    cols = columns(device % CHIPS, device // CHIPS)
    per_group = CHIPS // 4
    rows = jnp.concatenate(
        [columns(per_group * (group % 4) + q, group // 4) for q in range(per_group)], axis=1
    )
    gram_ref[...] = (
        lax.dot_general(rows, cols, TN, precision=EXACT, preferred_element_type=jnp.float32)
        / examples
    )
    kernel = lax.dot_general(
        full[...], full[...], NT, precision=EXACT, preferred_element_type=jnp.float32
    )
    sub = lax.broadcasted_iota(jnp.int32, kernel.shape, 0)
    lane = lax.broadcasted_iota(jnp.int32, kernel.shape, 1)
    diagonal = sub == lane
    ridge = jnp.sum(jnp.where(diagonal, kernel, 0.0)) / examples
    matrix = jnp.where(diagonal, kernel + ridge, kernel)
    for k in range(examples):
        column = matrix[:, k : k + 1]
        pivot = matrix[k : k + 1, k : k + 1]
        row = jnp.where(lane[:1] == k, 1.0, matrix[k : k + 1, :]) / pivot
        cleared = jnp.where(lane == k, 0.0, matrix) - column * row
        matrix = jnp.where(sub == k, row, cleared)
    inverse = jnp.sum(jnp.where(diagonal, matrix, 0.0), axis=0, keepdims=True)
    scores_ref[...] = 1.0 - ridge * inverse


def body(hidden_act, grad_output, down_weight, proj_in, proj_out, example_ids):
    group_count = lax.axis_size("grp")
    examples = EX_GRP * group_count
    device = lax.axis_index("fsdp")
    core = device % CORES
    plane = device // (RING * CORES)
    z = (device // CORES) % RING
    info = jnp.stack([core, device, lax.axis_index("grp")]).astype(jnp.int32)
    grad_rows = grad_output[0]
    tie = lax.optimization_barrier

    def chip(side, offset):
        return side * RING + (z + offset) % RING

    def columns(out, blocks):
        made = [((rows, permute(rows, SWAP)), chip(side, at)) for rows, side, at in blocks]
        return matmul_blocks(
            down_weight, [m[0] for m in made], [m[1] for m in made], core, out, TOK_GRP
        )

    near, away = plane, 1 - plane
    below1 = permute(grad_rows, UP)
    above1 = permute(grad_rows, DOWN)
    far0 = permute(grad_rows, ACROSS)
    hidden = jnp.transpose(hidden_act[0])
    kept, given = call(
        project_kernel,
        "project",
        10,
        (f32(HALF, TOK_GRP + LANES),) * 2,
        [
            info,
            *map(in_hbm, [hidden, jnp.transpose(proj_in), grad_rows, jnp.transpose(proj_out)]),
        ],
        [
            pltpu.VMEM(hidden.shape, jnp.bfloat16),
            pltpu.VMEM(proj_in.shape[::-1], jnp.bfloat16),
            pltpu.VMEM(grad_rows.shape, jnp.bfloat16),
            pltpu.VMEM(proj_out.shape[::-1], jnp.bfloat16),
            pltpu.VMEM((PROJ, TOK_GRP + LANES), jnp.float32),
            pltpu.SemaphoreType.DMA((7,)),
        ],
        [SMEM] + [ANY] * 4,
    )
    packed = call(
        pack_kernel, "pack", 6, f32(CHIPS, PROJ, LANES), [info, kept, permute(given, SWAP)]
    )
    below1, above1, far0, packed = tie((below1, above1, far0, packed))

    below2 = permute(below1, UP)
    above2 = permute(above1, DOWN)
    far_above1 = permute(above1, ACROSS)
    packed = lax.all_to_all(packed, "fsdp", 0, 0, axis_index_groups=SAME_CORE, tiled=True)
    out = columns(
        None, [(grad_rows, near, 0), (below1, near, -1), (above1, near, 1), (far0, away, 0)]
    )
    below2, above2, far_above1, out = tie((below2, above2, far_above1, out))

    below3 = permute(below2, UP)
    above3 = permute(above2, DOWN)
    far_below1 = permute(below1, ACROSS)
    left = call(left_kernel, "left", 4, f32(HALF, LANES), [info, packed])
    feats = call(
        feats_kernel,
        "feats",
        6,
        f32(CHIPS, EX_GRP, LANES),
        [info, packed, left, permute(left, SWAP), example_ids],
        [pltpu.VMEM((4 * EX_GRP, TOK_GRP), jnp.float32), pltpu.VMEM((HALF, TOK_GRP), jnp.float32)],
    )
    below3, above3, far_below1, feats = tie((below3, above3, far_below1, feats))

    far_below2 = permute(far_below1, UP)
    above4 = permute(above3, DOWN)
    far_above2 = permute(above2, ACROSS)
    feats = lax.all_to_all(feats, "fsdp", 0, 0, axis_index_groups=SAME_CORE, tiled=True)
    out = columns(
        out, [(below2, near, -2), (above2, near, 2), (far_above1, away, 1), (below3, near, -3)]
    )
    far_below2, above4, far_above2, out, feats = tie((far_below2, above4, far_above2, out, feats))

    far_below3 = permute(far_below2, UP)
    far_above3 = permute(far_above2, DOWN)
    far_above4 = permute(above4, ACROSS)
    feats = lax.all_to_all(
        jnp.broadcast_to(
            feats.reshape(1, CHIPS * EX_GRP, LANES), (group_count, CHIPS * EX_GRP, LANES)
        ),
        "grp",
        0,
        0,
        tiled=True,
    )
    out = columns(
        out,
        [(above3, near, 3), (far_below1, away, -1), (far_below2, away, -2), (above4, near, 4)],
    )
    far_below3, far_above3, far_above4, out, feats = tie(
        (far_below3, far_above3, far_above4, out, feats)
    )
    out = columns(
        out,
        [
            (far_above2, away, 2),
            (far_below3, away, -3),
            (far_above3, away, 3),
            (far_above4, away, 4),
        ],
    )
    gram, scores = call(
        functools.partial(finish_kernel, examples),
        "finish",
        12,
        (f32(PROJ * PROJ // group_count, LANES), f32(1, examples)),
        [info, feats, permute(feats, SWAP)],
        [pltpu.VMEM((examples, PROJ * PROJ), jnp.float32)],
    )
    return (jnp.transpose(out)[None], gram, scores[0])


def solution(mesh):
    in_specs = (
        P("grp", None, "fsdp"),
        P("grp", "fsdp", None),
        P("fsdp", None),
        P("fsdp", None),
        P(),
        P("grp", None),
    )
    out_specs = (P("grp", None, "fsdp"), P("grp", "fsdp"), P())
    return jax.shard_map(body, mesh=mesh, in_specs=in_specs, out_specs=out_specs, check_vma=False)
```

```python
import functools

import jax
import jax.numpy as jnp
from jax import lax
from jax.experimental import pallas as pl
from jax.experimental.pallas import tpu as pltpu
from jax.sharding import PartitionSpec as P

PROJ = 64
TOK_GRP = 2048
EX_GRP = 8
LANES = 128
PLANES = 2
RING = 8
CORES = 2
CHIPS = PLANES * RING
SAME_CORE = [[chip * CORES + core for chip in range(CHIPS)] for core in range(CORES)]
HALF = PROJ // CORES
NT = (((1,), (1,)), ((), ()))
TN = (((0,), (0,)), ((), ()))
NN = (((1,), (0,)), ((), ()))
EXACT = lax.Precision.HIGHEST
VMEM = pl.BlockSpec(memory_space=pltpu.VMEM)
SMEM = pl.BlockSpec(memory_space=pltpu.SMEM)
ANY = pl.BlockSpec(memory_space=pltpu.HBM)


def device_perm(move):
    pairs = []
    for plane in range(PLANES):
        for z in range(RING):
            for core in range(CORES):
                to_plane, to_z, to_core = move(plane, z, core)
                pairs.append(
                    (
                        (plane * RING + z) * CORES + core,
                        (to_plane * RING + to_z % RING) * CORES + to_core,
                    )
                )
    return pairs


UP = device_perm(lambda plane, z, core: (plane, z + 1, core))
DOWN = device_perm(lambda plane, z, core: (plane, z - 1, core))
ACROSS = device_perm(lambda plane, z, core: (1 - plane, z, core))
SWAP = device_perm(lambda plane, z, core: (plane, z, 1 - core))


def permute(value, pairs):
    return lax.ppermute(value, "fsdp", pairs)


def call(
    kernel, name, room, out_shape, args, scratch=(), in_specs=None, out_specs=None, aliases=None
):
    return pl.pallas_call(
        kernel,
        name=name,
        out_shape=out_shape,
        in_specs=in_specs or [SMEM] + [VMEM] * (len(args) - 1),
        out_specs=out_specs
        or (VMEM if not isinstance(out_shape, tuple) else (VMEM,) * len(out_shape)),
        scratch_shapes=list(scratch),
        input_output_aliases=aliases or {},
        compiler_params=pltpu.CompilerParams(vmem_limit_bytes=room << 20),
        cost_estimate=pl.CostEstimate(flops=0, transcendentals=0, bytes_accessed=0),
    )(*args)


def in_hbm(value):
    return pltpu.with_memory_space_constraint(value, pltpu.HBM)


def f32(*shape):
    return jax.ShapeDtypeStruct(shape, jnp.float32)


def matmul_kernel(count, place_ref, weight_hbm, *refs):
    block_refs = refs[: 2 * count]
    out_ref, weight, rows, rounded, weight_sems, row_sems, out_sems = refs[-7:]
    core = place_ref[count]
    wide = 2 * LANES
    height = weight_hbm.shape[0] // 2
    weights = [
        pltpu.make_async_copy(
            weight_hbm.at[pl.ds(i * height, height)],
            weight.at[pl.ds(i * height, height)],
            weight_sems.at[i],
        )
        for i in range(2)
    ]
    for load in weights:
        load.start()
    for b in range(count):
        for side, half in enumerate((core, 1 - core)):
            start = pl.multiple_of(b * LANES + half * 64, 64)
            pltpu.make_async_copy(
                block_refs[2 * b + side], rows.at[pl.ds(start, 64)], row_sems.at[2 * b + side]
            ).start()
    for load in weights:
        load.wait()

    def store(i, b):
        column = pl.multiple_of(place_ref[2 * i + b] * LANES, LANES)
        return pltpu.make_async_copy(
            rounded.at[i, :, pl.ds(b * LANES, LANES)],
            out_ref.at[:, pl.ds(column, LANES)],
            out_sems.at[2 * i + b],
        )

    def pair(i, carry):
        start = pl.multiple_of(i * wide, wide)
        for quarter in range(4):
            pltpu.make_async_copy(
                block_refs[0], rows.at[pl.ds(start + quarter * 64, 64)], row_sems.at[4 * i + quarter]
            ).wait()
        rounded[i] = lax.dot_general(
            weight[...], rows[pl.ds(start, wide), :], NT, preferred_element_type=jnp.float32
        ).astype(jnp.bfloat16)
        for b in range(2):
            store(i, b).start()
        return carry

    lax.fori_loop(0, count // 2, pair, 0)
    for b in range(count):
        store(b // 2, b % 2).wait()


def matmul_blocks(weight, blocks, places, core, out, tokens):
    count = len(blocks)
    width, depth = weight.shape
    flat = [array for pair in blocks for array in pair]
    args = [jnp.stack([*places, core]).astype(jnp.int32), *map(in_hbm, [weight, *flat])]
    aliases = {}
    if out is not None:
        args.append(out)
        aliases = {len(args) - 1: 0}
    return call(
        functools.partial(matmul_kernel, count),
        "grad_columns",
        14,
        jax.ShapeDtypeStruct((width, tokens), jnp.bfloat16),
        args,
        [
            pltpu.VMEM((width, depth), jnp.bfloat16),
            pltpu.VMEM((count * LANES, depth), jnp.bfloat16),
            pltpu.VMEM((count // 2, width, 2 * LANES), jnp.bfloat16),
            pltpu.SemaphoreType.DMA((2,)),
            pltpu.SemaphoreType.DMA((2 * count,)),
            pltpu.SemaphoreType.DMA((count,)),
        ],
        [SMEM] + [ANY] * (len(args) - 1),
        ANY,
        aliases,
    )


def project_kernel(
    info_ref, hidden_hbm, proj_in_hbm, rows_hbm, proj_out_hbm, kept_ref, given_ref,
    hidden, proj_in, rows, proj_out, both, sems
):
    core = info_ref[0]
    parts = 4
    width = TOK_GRP // parts
    chunks = [
        pltpu.make_async_copy(
            hidden_hbm.at[:, pl.ds(i * width, width)],
            hidden.at[:, pl.ds(i * width, width)],
            sems.at[i],
        )
        for i in range(parts)
    ]
    small = [
        pltpu.make_async_copy(source, target, sems.at[parts + i])
        for i, (source, target) in enumerate(
            ((proj_in_hbm, proj_in), (rows_hbm, rows), (proj_out_hbm, proj_out))
        )
    ]
    for load in (small[0], *chunks, small[1], small[2]):
        load.start()
    small[0].wait()
    for i in range(parts):
        chunks[i].wait()
        lanes = slice(i * width, (i + 1) * width)
        both[:, lanes] = lax.dot_general(
            proj_in[...], hidden[:, lanes], NN, preferred_element_type=jnp.float32
        )
    small[1].wait()
    small[2].wait()
    right = lax.dot_general(proj_out[...], rows[...], NT, preferred_element_type=jnp.float32)
    both[:, TOK_GRP:] = jnp.concatenate([right, jnp.zeros_like(right)], axis=1)
    kept_ref[...] = both[pl.ds(pl.multiple_of(core * HALF, HALF), HALF), :]
    given_ref[...] = both[pl.ds(pl.multiple_of((1 - core) * HALF, HALF), HALF), :]


def pack_kernel(info_ref, kept_ref, taken_ref, out_ref):
    core = info_ref[0]
    for block in range(TOK_GRP // LANES):
        lanes = slice(block * LANES, (block + 1) * LANES)
        total = kept_ref[:, lanes] + taken_ref[:, lanes]
        out_ref[:, 2 * block : 2 * block + 2, :] = total.reshape(CHIPS, 2, LANES)
    kept = kept_ref[:, TOK_GRP : TOK_GRP + 64]
    taken = taken_ref[:, TOK_GRP : TOK_GRP + 64]
    right = jnp.where(
        core == 0,
        jnp.concatenate([kept, taken], axis=1),
        jnp.concatenate([taken, kept], axis=1),
    )
    out_ref[:, HALF:, :] = jnp.broadcast_to(right[None], (CHIPS, HALF, LANES))


def left_kernel(info_ref, packed_ref, out_ref):
    total = packed_ref[0, :HALF, :]
    for chip in range(1, CHIPS):
        total += packed_ref[chip, :HALF, :]
    out_ref[...] = total


def feats_kernel(info_ref, packed_ref, left_ref, other_ref, ids_ref, out_ref, weighted, right):
    core = info_ref[0]
    low = jnp.where(core == 0, left_ref[...], other_ref[...])
    high = jnp.where(core == 0, other_ref[...], left_ref[...])
    example = lax.broadcasted_iota(jnp.int32, (EX_GRP, LANES), 0)
    for block in range(TOK_GRP // LANES):
        lanes = slice(block * LANES, (block + 1) * LANES)
        mine = ids_ref[:, lanes] == example
        for column in range(4):
            source = low if column < 2 else high
            row = 2 * block + column % 2
            weighted[column * EX_GRP : (column + 1) * EX_GRP, lanes] = jnp.where(
                mine, source[row : row + 1, :], 0.0
            )
        right[:, lanes] = packed_ref[block, HALF:, :]
    sums = lax.dot_general(
        weighted[...], right[...], NT, precision=EXACT, preferred_element_type=jnp.float32
    )
    sums = sums * (EX_GRP / TOK_GRP) ** 0.5
    wide = jnp.concatenate(
        [sums[c * EX_GRP : (c + 1) * EX_GRP, :] for c in range(4)], axis=1
    )
    out_ref[...] = jnp.broadcast_to(wide[None], out_ref.shape)


def finish_kernel(examples, count, info_ref, place_ref, mine_ref, other_ref, weight_hbm, *refs):
    block_refs = refs[: 2 * count]
    out_ref, gram_ref, scores_ref, full, weight, tokens, total, rounded, load_sems, out_sems = refs[
        2 * count + 1 :
    ]
    loads = [pltpu.make_async_copy(weight_hbm, weight, load_sems.at[2 * count])]
    for b in range(count):
        for side in range(2):
            half = info_ref[0] if side == 0 else 1 - info_ref[0]
            start = pl.multiple_of(b * LANES + half * 64, 64)
            loads.append(
                pltpu.make_async_copy(
                    block_refs[2 * b + side], tokens.at[pl.ds(start, 64)], load_sems.at[2 * b + side]
                )
            )
    for load in loads:
        load.start()
    core, device, group = info_ref[0], info_ref[1], info_ref[2]
    for chip in range(CHIPS):
        rows = slice(chip * EX_GRP, (chip + 1) * EX_GRP)
        for part, ref in enumerate((mine_ref, other_ref)):
            start = (part * CHIPS + chip) * LANES
            full[:, start : start + LANES] = ref[:, rows, :].reshape(examples, LANES)

    def columns(chip, upper):
        start = pl.multiple_of(chip * EX_GRP, EX_GRP)
        halves = []
        for ref in (mine_ref, other_ref):
            part = ref[:, pl.ds(start, EX_GRP), :].reshape(examples, LANES)
            halves.append(jnp.where(upper == 0, part[:, :64], part[:, 64:]))
        first = jnp.where(core == 0, halves[0], halves[1])
        second = jnp.where(core == 0, halves[1], halves[0])
        return jnp.concatenate(
            [first[:, :HALF], second[:, :HALF], first[:, HALF:], second[:, HALF:]], axis=1
        )

    cols = columns(device % CHIPS, device // CHIPS)
    per_group = CHIPS // 4
    gram_rows = jnp.concatenate(
        [columns(per_group * (group % 4) + q, group // 4) for q in range(per_group)], axis=1
    )
    gram_ref[...] = (
        lax.dot_general(gram_rows, cols, TN, precision=EXACT, preferred_element_type=jnp.float32)
        / examples
    )
    kernel = lax.dot_general(
        full[...], full[...], NT, precision=EXACT, preferred_element_type=jnp.float32
    )
    sub = lax.broadcasted_iota(jnp.int32, kernel.shape, 0)
    lane = lax.broadcasted_iota(jnp.int32, kernel.shape, 1)
    diagonal = sub == lane
    ridge = jnp.sum(jnp.where(diagonal, kernel, 0.0)) / examples
    matrix = jnp.where(diagonal, kernel + ridge, kernel)
    for load in loads:
        load.wait()
    pieces = 8
    depth = weight.shape[1] // pieces
    for piece in range(pieces):
        part = slice(piece * depth, (piece + 1) * depth)
        product = lax.dot_general(
            weight[:, part], tokens[:, part], NT, preferred_element_type=jnp.float32
        )
        if piece == 0:
            total[...] = product
        elif piece < pieces - 1:
            total[...] += product
        else:
            rounded[...] = (total[...] + product).astype(jnp.bfloat16)
        for k in range(piece * examples // pieces, (piece + 1) * examples // pieces):
            column = matrix[:, k : k + 1]
            pivot = matrix[k : k + 1, k : k + 1]
            row = jnp.where(lane[:1] == k, 1.0, matrix[k : k + 1, :]) / pivot
            cleared = jnp.where(lane == k, 0.0, matrix) - column * row
            matrix = jnp.where(sub == k, row, cleared)
    stores = []
    for b in range(count):
        place = pl.multiple_of(place_ref[b] * LANES, LANES)
        stores.append(
            pltpu.make_async_copy(
                rounded.at[:, pl.ds(b * LANES, LANES)],
                out_ref.at[:, pl.ds(place, LANES)],
                out_sems.at[b],
            )
        )
    for store in stores:
        store.start()
    inverse = jnp.sum(jnp.where(diagonal, matrix, 0.0), axis=0, keepdims=True)
    scores_ref[...] = 1.0 - ridge * inverse
    for store in stores:
        store.wait()


def body(hidden_act, grad_output, down_weight, proj_in, proj_out, example_ids):
    group_count = lax.axis_size("grp")
    examples = EX_GRP * group_count
    device = lax.axis_index("fsdp")
    core = device % CORES
    plane = device // (RING * CORES)
    z = (device // CORES) % RING
    info = jnp.stack([core, device, lax.axis_index("grp")]).astype(jnp.int32)
    grad_rows = grad_output[0]
    tie = lax.optimization_barrier

    def chip(side, offset):
        return side * RING + (z + offset) % RING

    def columns(out, blocks):
        made = [((rows, permute(rows, SWAP)), chip(side, at)) for rows, side, at in blocks]
        return matmul_blocks(
            down_weight, [m[0] for m in made], [m[1] for m in made], core, out, TOK_GRP
        )

    near, away = plane, 1 - plane
    below1 = permute(grad_rows, UP)
    above1 = permute(grad_rows, DOWN)
    far0 = permute(grad_rows, ACROSS)
    hidden = jnp.transpose(hidden_act[0])
    kept, given = call(
        project_kernel,
        "project",
        10,
        (f32(HALF, TOK_GRP + LANES),) * 2,
        [
            info,
            *map(in_hbm, [hidden, jnp.transpose(proj_in), grad_rows, jnp.transpose(proj_out)]),
        ],
        [
            pltpu.VMEM(hidden.shape, jnp.bfloat16),
            pltpu.VMEM(proj_in.shape[::-1], jnp.bfloat16),
            pltpu.VMEM(grad_rows.shape, jnp.bfloat16),
            pltpu.VMEM(proj_out.shape[::-1], jnp.bfloat16),
            pltpu.VMEM((PROJ, TOK_GRP + LANES), jnp.float32),
            pltpu.SemaphoreType.DMA((7,)),
        ],
        [SMEM] + [ANY] * 4,
    )
    packed = call(
        pack_kernel, "pack", 6, f32(CHIPS, PROJ, LANES), [info, kept, permute(given, SWAP)]
    )
    below1, above1, far0, packed = tie((below1, above1, far0, packed))

    below2 = permute(below1, UP)
    above2 = permute(above1, DOWN)
    far_above1 = permute(above1, ACROSS)
    packed = lax.all_to_all(packed, "fsdp", 0, 0, axis_index_groups=SAME_CORE, tiled=True)
    out = columns(
        None, [(grad_rows, near, 0), (below1, near, -1), (above1, near, 1), (far0, away, 0)]
    )
    below2, above2, far_above1, out = tie((below2, above2, far_above1, out))

    below3 = permute(below2, UP)
    above3 = permute(above2, DOWN)
    far_below1 = permute(below1, ACROSS)
    left = call(left_kernel, "left", 4, f32(HALF, LANES), [info, packed])
    feats = call(
        feats_kernel,
        "feats",
        6,
        f32(CHIPS, EX_GRP, LANES),
        [info, packed, left, permute(left, SWAP), example_ids],
        [pltpu.VMEM((4 * EX_GRP, TOK_GRP), jnp.float32), pltpu.VMEM((HALF, TOK_GRP), jnp.float32)],
    )
    below3, above3, far_below1, feats = tie((below3, above3, far_below1, feats))

    far_below2 = permute(far_below1, UP)
    above4 = permute(above3, DOWN)
    far_above2 = permute(above2, ACROSS)
    feats = lax.all_to_all(feats, "fsdp", 0, 0, axis_index_groups=SAME_CORE, tiled=True)
    out = columns(
        out, [(below2, near, -2), (above2, near, 2), (far_above1, away, 1), (below3, near, -3)]
    )
    far_below2, above4, far_above2, out, feats = tie((far_below2, above4, far_above2, out, feats))

    far_below3 = permute(far_below2, UP)
    far_above3 = permute(far_above2, DOWN)
    far_above4 = permute(above4, ACROSS)
    feats = lax.all_to_all(
        jnp.broadcast_to(
            feats.reshape(1, CHIPS * EX_GRP, LANES), (group_count, CHIPS * EX_GRP, LANES)
        ),
        "grp",
        0,
        0,
        tiled=True,
    )
    out = columns(
        out,
        [(above3, near, 3), (far_below1, away, -1), (far_below2, away, -2), (above4, near, 4)],
    )
    far_below3, far_above3, far_above4, out, feats = tie(
        (far_below3, far_above3, far_above4, out, feats)
    )
    last = [
        (far_above2, chip(away, 2)),
        (far_below3, chip(away, -3)),
        (far_above3, chip(away, 3)),
        (far_above4, chip(away, 4)),
    ]
    pairs = [rows for block, _ in last for rows in (block, permute(block, SWAP))]
    args = [info, jnp.stack([place for _, place in last]).astype(jnp.int32), feats]
    args += [permute(feats, SWAP), *map(in_hbm, [down_weight, *pairs]), out]
    width, depth = down_weight.shape
    wide = len(last) * LANES
    out, gram, scores = call(
        functools.partial(finish_kernel, examples, len(last)),
        "finish",
        18,
        (
            jax.ShapeDtypeStruct(out.shape, out.dtype),
            f32(PROJ * PROJ // group_count, LANES),
            f32(1, examples),
        ),
        args,
        [
            pltpu.VMEM((examples, PROJ * PROJ), jnp.float32),
            pltpu.VMEM((width, depth), jnp.bfloat16),
            pltpu.VMEM((wide, depth), jnp.bfloat16),
            pltpu.VMEM((width, wide), jnp.float32),
            pltpu.VMEM((width, wide), jnp.bfloat16),
            pltpu.SemaphoreType.DMA((2 * len(last) + 1,)),
            pltpu.SemaphoreType.DMA((len(last),)),
        ],
        [SMEM, SMEM, VMEM, VMEM] + [ANY] * (len(pairs) + 2),
        (ANY, VMEM, VMEM),
        {len(args) - 1: 0},
    )
    return (jnp.transpose(out)[None], gram, scores[0])


def solution(mesh):
    in_specs = (
        P("grp", None, "fsdp"),
        P("grp", "fsdp", None),
        P("fsdp", None),
        P("fsdp", None),
        P(),
        P("grp", None),
    )
    out_specs = (P("grp", None, "fsdp"), P("grp", "fsdp"), P())
    return jax.shard_map(body, mesh=mesh, in_specs=in_specs, out_specs=out_specs, check_vma=False)
```

```python
import functools

import jax
import jax.numpy as jnp
from jax import lax
from jax.experimental import pallas as pl
from jax.experimental.pallas import tpu as pltpu
from jax.sharding import PartitionSpec as P

PROJ = 64
TOK_GRP = 2048
EX_GRP = 8
LANES = 128
PLANES = 2
RING = 8
CORES = 2
CHIPS = PLANES * RING
SAME_CORE = [[chip * CORES + core for chip in range(CHIPS)] for core in range(CORES)]
HALF = PROJ // CORES
NT = (((1,), (1,)), ((), ()))
TN = (((0,), (0,)), ((), ()))
NN = (((1,), (0,)), ((), ()))
EXACT = lax.Precision.HIGHEST
VMEM = pl.BlockSpec(memory_space=pltpu.VMEM)
SMEM = pl.BlockSpec(memory_space=pltpu.SMEM)
ANY = pl.BlockSpec(memory_space=pltpu.HBM)


def device_perm(move):
    pairs = []
    for plane in range(PLANES):
        for z in range(RING):
            for core in range(CORES):
                to_plane, to_z, to_core = move(plane, z, core)
                pairs.append(
                    (
                        (plane * RING + z) * CORES + core,
                        (to_plane * RING + to_z % RING) * CORES + to_core,
                    )
                )
    return pairs


UP = device_perm(lambda plane, z, core: (plane, z + 1, core))
DOWN = device_perm(lambda plane, z, core: (plane, z - 1, core))
ACROSS = device_perm(lambda plane, z, core: (1 - plane, z, core))
SWAP = device_perm(lambda plane, z, core: (plane, z, 1 - core))


def permute(value, pairs):
    return lax.ppermute(value, "fsdp", pairs)


def call(
    kernel, name, room, out_shape, args, scratch=(), in_specs=None, out_specs=None, aliases=None
):
    return pl.pallas_call(
        kernel,
        name=name,
        out_shape=out_shape,
        in_specs=in_specs or [SMEM] + [VMEM] * (len(args) - 1),
        out_specs=out_specs
        or (VMEM if not isinstance(out_shape, tuple) else (VMEM,) * len(out_shape)),
        scratch_shapes=list(scratch),
        input_output_aliases=aliases or {},
        compiler_params=pltpu.CompilerParams(vmem_limit_bytes=room << 20),
        cost_estimate=pl.CostEstimate(flops=0, transcendentals=0, bytes_accessed=0),
    )(*args)


def in_hbm(value):
    return pltpu.with_memory_space_constraint(value, pltpu.HBM)


def f32(*shape):
    return jax.ShapeDtypeStruct(shape, jnp.float32)


def matmul_kernel(count, place_ref, weight_hbm, *refs):
    block_refs = refs[: 2 * count]
    out_ref, weight, rows, rounded, weight_sems, row_sems, out_sems = refs[-7:]
    core = place_ref[count]
    wide = 2 * LANES
    height = weight_hbm.shape[0] // 2
    weights = [
        pltpu.make_async_copy(
            weight_hbm.at[pl.ds(i * height, height)],
            weight.at[pl.ds(i * height, height)],
            weight_sems.at[i],
        )
        for i in range(2)
    ]
    for load in weights:
        load.start()
    for b in range(count):
        for side, half in enumerate((core, 1 - core)):
            start = pl.multiple_of(b * LANES + half * 64, 64)
            pltpu.make_async_copy(
                block_refs[2 * b + side], rows.at[pl.ds(start, 64)], row_sems.at[2 * b + side]
            ).start()
    for load in weights:
        load.wait()

    def store(i, b):
        column = pl.multiple_of(place_ref[2 * i + b] * LANES, LANES)
        return pltpu.make_async_copy(
            rounded.at[i, :, pl.ds(b * LANES, LANES)],
            out_ref.at[:, pl.ds(column, LANES)],
            out_sems.at[2 * i + b],
        )

    def pair(i, carry):
        start = pl.multiple_of(i * wide, wide)
        for quarter in range(4):
            pltpu.make_async_copy(
                block_refs[0], rows.at[pl.ds(start + quarter * 64, 64)], row_sems.at[4 * i + quarter]
            ).wait()
        rounded[i] = lax.dot_general(
            weight[...], rows[pl.ds(start, wide), :], NT, preferred_element_type=jnp.float32
        ).astype(jnp.bfloat16)
        for b in range(2):
            store(i, b).start()
        return carry

    lax.fori_loop(0, count // 2, pair, 0)
    for b in range(count):
        store(b // 2, b % 2).wait()


def matmul_blocks(weight, blocks, places, core, out, tokens):
    count = len(blocks)
    width, depth = weight.shape
    flat = [array for pair in blocks for array in pair]
    args = [jnp.stack([*places, core]).astype(jnp.int32), *map(in_hbm, [weight, *flat])]
    aliases = {}
    if out is not None:
        args.append(out)
        aliases = {len(args) - 1: 0}
    return call(
        functools.partial(matmul_kernel, count),
        "grad_columns",
        14,
        jax.ShapeDtypeStruct((width, tokens), jnp.bfloat16),
        args,
        [
            pltpu.VMEM((width, depth), jnp.bfloat16),
            pltpu.VMEM((count * LANES, depth), jnp.bfloat16),
            pltpu.VMEM((count // 2, width, 2 * LANES), jnp.bfloat16),
            pltpu.SemaphoreType.DMA((2,)),
            pltpu.SemaphoreType.DMA((2 * count,)),
            pltpu.SemaphoreType.DMA((count,)),
        ],
        [SMEM] + [ANY] * (len(args) - 1),
        ANY,
        aliases,
    )


def project_kernel(
    info_ref, hidden_hbm, proj_in_hbm, rows_hbm, proj_out_hbm, kept_ref, given_ref,
    hidden, proj_in, rows, proj_out, both, sems
):
    core = info_ref[0]
    parts = 4
    width = TOK_GRP // parts
    chunks = [
        pltpu.make_async_copy(
            hidden_hbm.at[:, pl.ds(i * width, width)],
            hidden.at[:, pl.ds(i * width, width)],
            sems.at[i],
        )
        for i in range(parts)
    ]
    small = [
        pltpu.make_async_copy(source, target, sems.at[parts + i])
        for i, (source, target) in enumerate(
            ((proj_in_hbm, proj_in), (rows_hbm, rows), (proj_out_hbm, proj_out))
        )
    ]
    for load in (small[0], *chunks, small[1], small[2]):
        load.start()
    small[0].wait()
    for i in range(parts):
        chunks[i].wait()
        lanes = slice(i * width, (i + 1) * width)
        both[:, lanes] = lax.dot_general(
            proj_in[...], hidden[:, lanes], NN, preferred_element_type=jnp.float32
        )
    small[1].wait()
    small[2].wait()
    right = lax.dot_general(proj_out[...], rows[...], NT, preferred_element_type=jnp.float32)
    both[:, TOK_GRP:] = jnp.concatenate([right, jnp.zeros_like(right)], axis=1)
    kept_ref[...] = both[pl.ds(pl.multiple_of(core * HALF, HALF), HALF), :]
    given_ref[...] = both[pl.ds(pl.multiple_of((1 - core) * HALF, HALF), HALF), :]


def pack_kernel(info_ref, kept_ref, taken_ref, out_ref):
    core = info_ref[0]
    for block in range(TOK_GRP // LANES):
        lanes = slice(block * LANES, (block + 1) * LANES)
        total = kept_ref[:, lanes] + taken_ref[:, lanes]
        out_ref[:, 2 * block : 2 * block + 2, :] = total.reshape(CHIPS, 2, LANES)
    kept = kept_ref[:, TOK_GRP : TOK_GRP + 64]
    taken = taken_ref[:, TOK_GRP : TOK_GRP + 64]
    right = jnp.where(
        core == 0,
        jnp.concatenate([kept, taken], axis=1),
        jnp.concatenate([taken, kept], axis=1),
    )
    out_ref[:, HALF:, :] = jnp.broadcast_to(right[None], (CHIPS, HALF, LANES))


def left_kernel(info_ref, packed_ref, out_ref):
    total = packed_ref[0, :HALF, :]
    for chip in range(1, CHIPS):
        total += packed_ref[chip, :HALF, :]
    out_ref[...] = total


def feats_kernel(info_ref, packed_ref, left_ref, other_ref, ids_ref, out_ref, weighted, right):
    core = info_ref[0]
    low = jnp.where(core == 0, left_ref[...], other_ref[...])
    high = jnp.where(core == 0, other_ref[...], left_ref[...])
    example = lax.broadcasted_iota(jnp.int32, (EX_GRP, LANES), 0)
    for block in range(TOK_GRP // LANES):
        lanes = slice(block * LANES, (block + 1) * LANES)
        mine = ids_ref[:, lanes] == example
        for column in range(4):
            source = low if column < 2 else high
            row = 2 * block + column % 2
            weighted[column * EX_GRP : (column + 1) * EX_GRP, lanes] = jnp.where(
                mine, source[row : row + 1, :], 0.0
            )
        right[:, lanes] = packed_ref[block, HALF:, :]
    sums = lax.dot_general(
        weighted[...], right[...], NT, precision=EXACT, preferred_element_type=jnp.float32
    )
    sums = sums * (EX_GRP / TOK_GRP) ** 0.5
    wide = jnp.concatenate(
        [sums[c * EX_GRP : (c + 1) * EX_GRP, :] for c in range(4)], axis=1
    )
    out_ref[...] = jnp.broadcast_to(wide[None], out_ref.shape)


def finish_kernel(examples, count, info_ref, place_ref, mine_ref, other_ref, weight_hbm, *refs):
    block_refs = refs[: 2 * count]
    out_ref, gram_ref, scores_ref, full, weight, tokens, total, rounded, load_sems, out_sems = refs[
        2 * count + 1 :
    ]
    loads = [pltpu.make_async_copy(weight_hbm, weight, load_sems.at[2 * count])]
    for b in range(count):
        for side in range(2):
            half = info_ref[0] if side == 0 else 1 - info_ref[0]
            start = pl.multiple_of(b * LANES + half * 64, 64)
            loads.append(
                pltpu.make_async_copy(
                    block_refs[2 * b + side], tokens.at[pl.ds(start, 64)], load_sems.at[2 * b + side]
                )
            )
    for load in loads:
        load.start()
    core, device, group = info_ref[0], info_ref[1], info_ref[2]
    for chip in range(CHIPS):
        rows = slice(chip * EX_GRP, (chip + 1) * EX_GRP)
        for part, ref in enumerate((mine_ref, other_ref)):
            start = (part * CHIPS + chip) * LANES
            part_rows = ref[:, rows, :].reshape(examples, LANES)
            full[:, start : start + LANES] = part_rows.astype(jnp.bfloat16)

    def columns(chip, upper):
        start = pl.multiple_of(chip * EX_GRP, EX_GRP)
        halves = []
        for ref in (mine_ref, other_ref):
            part = ref[:, pl.ds(start, EX_GRP), :].reshape(examples, LANES)
            halves.append(jnp.where(upper == 0, part[:, :64], part[:, 64:]))
        first = jnp.where(core == 0, halves[0], halves[1])
        second = jnp.where(core == 0, halves[1], halves[0])
        return jnp.concatenate(
            [first[:, :HALF], second[:, :HALF], first[:, HALF:], second[:, HALF:]], axis=1
        )

    cols = columns(device % CHIPS, device // CHIPS)
    per_group = CHIPS // 4
    gram_rows = jnp.concatenate(
        [columns(per_group * (group % 4) + q, group // 4) for q in range(per_group)], axis=1
    )
    gram_ref[...] = (
        lax.dot_general(gram_rows, cols, TN, precision=EXACT, preferred_element_type=jnp.float32)
        / examples
    )
    kernel = lax.dot_general(
        full[...], full[...], NT, preferred_element_type=jnp.float32
    )
    sub = lax.broadcasted_iota(jnp.int32, kernel.shape, 0)
    lane = lax.broadcasted_iota(jnp.int32, kernel.shape, 1)
    diagonal = sub == lane
    ridge = jnp.sum(jnp.where(diagonal, kernel, 0.0)) / examples
    matrix = jnp.where(diagonal, kernel + ridge, kernel)
    for load in loads:
        load.wait()
    pieces = 8
    depth = weight.shape[1] // pieces
    for piece in range(pieces):
        part = slice(piece * depth, (piece + 1) * depth)
        product = lax.dot_general(
            weight[:, part], tokens[:, part], NT, preferred_element_type=jnp.float32
        )
        if piece == 0:
            total[...] = product
        elif piece < pieces - 1:
            total[...] += product
        else:
            rounded[...] = (total[...] + product).astype(jnp.bfloat16)
        for k in range(piece * examples // pieces, (piece + 1) * examples // pieces):
            column = matrix[:, k : k + 1]
            pivot = matrix[k : k + 1, k : k + 1]
            row = jnp.where(lane[:1] == k, 1.0, matrix[k : k + 1, :]) / pivot
            cleared = jnp.where(lane == k, 0.0, matrix) - column * row
            matrix = jnp.where(sub == k, row, cleared)
    stores = []
    for b in range(count):
        place = pl.multiple_of(place_ref[b] * LANES, LANES)
        stores.append(
            pltpu.make_async_copy(
                rounded.at[:, pl.ds(b * LANES, LANES)],
                out_ref.at[:, pl.ds(place, LANES)],
                out_sems.at[b],
            )
        )
    for store in stores:
        store.start()
    inverse = jnp.sum(jnp.where(diagonal, matrix, 0.0), axis=0, keepdims=True)
    scores_ref[...] = 1.0 - ridge * inverse
    for store in stores:
        store.wait()


def body(hidden_act, grad_output, down_weight, proj_in, proj_out, example_ids):
    group_count = lax.axis_size("grp")
    examples = EX_GRP * group_count
    device = lax.axis_index("fsdp")
    core = device % CORES
    plane = device // (RING * CORES)
    z = (device // CORES) % RING
    info = jnp.stack([core, device, lax.axis_index("grp")]).astype(jnp.int32)
    grad_rows = grad_output[0]
    tie = lax.optimization_barrier

    def chip(side, offset):
        return side * RING + (z + offset) % RING

    def columns(out, blocks):
        made = [((rows, permute(rows, SWAP)), chip(side, at)) for rows, side, at in blocks]
        return matmul_blocks(
            down_weight, [m[0] for m in made], [m[1] for m in made], core, out, TOK_GRP
        )

    near, away = plane, 1 - plane
    below1 = permute(grad_rows, UP)
    above1 = permute(grad_rows, DOWN)
    far0 = permute(grad_rows, ACROSS)
    hidden = jnp.transpose(hidden_act[0])
    kept, given = call(
        project_kernel,
        "project",
        10,
        (f32(HALF, TOK_GRP + LANES),) * 2,
        [
            info,
            *map(in_hbm, [hidden, jnp.transpose(proj_in), grad_rows, jnp.transpose(proj_out)]),
        ],
        [
            pltpu.VMEM(hidden.shape, jnp.bfloat16),
            pltpu.VMEM(proj_in.shape[::-1], jnp.bfloat16),
            pltpu.VMEM(grad_rows.shape, jnp.bfloat16),
            pltpu.VMEM(proj_out.shape[::-1], jnp.bfloat16),
            pltpu.VMEM((PROJ, TOK_GRP + LANES), jnp.float32),
            pltpu.SemaphoreType.DMA((7,)),
        ],
        [SMEM] + [ANY] * 4,
    )
    packed = call(
        pack_kernel, "pack", 6, f32(CHIPS, PROJ, LANES), [info, kept, permute(given, SWAP)]
    )
    below1, above1, far0, packed = tie((below1, above1, far0, packed))

    below2 = permute(below1, UP)
    above2 = permute(above1, DOWN)
    far_above1 = permute(above1, ACROSS)
    packed = lax.all_to_all(packed, "fsdp", 0, 0, axis_index_groups=SAME_CORE, tiled=True)
    out = columns(
        None, [(grad_rows, near, 0), (below1, near, -1), (above1, near, 1), (far0, away, 0)]
    )
    below2, above2, far_above1, out = tie((below2, above2, far_above1, out))

    below3 = permute(below2, UP)
    above3 = permute(above2, DOWN)
    far_below1 = permute(below1, ACROSS)
    left = call(left_kernel, "left", 4, f32(HALF, LANES), [info, packed])
    feats = call(
        feats_kernel,
        "feats",
        6,
        f32(CHIPS, EX_GRP, LANES),
        [info, packed, left, permute(left, SWAP), example_ids],
        [pltpu.VMEM((4 * EX_GRP, TOK_GRP), jnp.float32), pltpu.VMEM((HALF, TOK_GRP), jnp.float32)],
    )
    below3, above3, far_below1, feats = tie((below3, above3, far_below1, feats))

    far_below2 = permute(far_below1, UP)
    above4 = permute(above3, DOWN)
    far_above2 = permute(above2, ACROSS)
    feats = lax.all_to_all(feats, "fsdp", 0, 0, axis_index_groups=SAME_CORE, tiled=True)
    out = columns(
        out, [(below2, near, -2), (above2, near, 2), (far_above1, away, 1), (below3, near, -3)]
    )
    far_below2, above4, far_above2, out, feats = tie((far_below2, above4, far_above2, out, feats))

    far_below3 = permute(far_below2, UP)
    far_above3 = permute(far_above2, DOWN)
    far_above4 = permute(above4, ACROSS)
    feats = lax.all_to_all(
        jnp.broadcast_to(
            feats.reshape(1, CHIPS * EX_GRP, LANES), (group_count, CHIPS * EX_GRP, LANES)
        ),
        "grp",
        0,
        0,
        tiled=True,
    )
    out = columns(
        out,
        [(above3, near, 3), (far_below1, away, -1), (far_below2, away, -2), (above4, near, 4)],
    )
    far_below3, far_above3, far_above4, out, feats = tie(
        (far_below3, far_above3, far_above4, out, feats)
    )
    last = [
        (far_above2, chip(away, 2)),
        (far_below3, chip(away, -3)),
        (far_above3, chip(away, 3)),
        (far_above4, chip(away, 4)),
    ]
    pairs = [rows for block, _ in last for rows in (block, permute(block, SWAP))]
    args = [info, jnp.stack([place for _, place in last]).astype(jnp.int32), feats]
    args += [permute(feats, SWAP), *map(in_hbm, [down_weight, *pairs]), out]
    width, depth = down_weight.shape
    wide = len(last) * LANES
    out, gram, scores = call(
        functools.partial(finish_kernel, examples, len(last)),
        "finish",
        18,
        (
            jax.ShapeDtypeStruct(out.shape, out.dtype),
            f32(PROJ * PROJ // group_count, LANES),
            f32(1, examples),
        ),
        args,
        [
            pltpu.VMEM((examples, PROJ * PROJ), jnp.bfloat16),
            pltpu.VMEM((width, depth), jnp.bfloat16),
            pltpu.VMEM((wide, depth), jnp.bfloat16),
            pltpu.VMEM((width, wide), jnp.float32),
            pltpu.VMEM((width, wide), jnp.bfloat16),
            pltpu.SemaphoreType.DMA((2 * len(last) + 1,)),
            pltpu.SemaphoreType.DMA((len(last),)),
        ],
        [SMEM, SMEM, VMEM, VMEM] + [ANY] * (len(pairs) + 2),
        (ANY, VMEM, VMEM),
        {len(args) - 1: 0},
    )
    return (jnp.transpose(out)[None], gram, scores[0])


def solution(mesh):
    in_specs = (
        P("grp", None, "fsdp"),
        P("grp", "fsdp", None),
        P("fsdp", None),
        P("fsdp", None),
        P(),
        P("grp", None),
    )
    out_specs = (P("grp", None, "fsdp"), P("grp", "fsdp"), P())
    return jax.shard_map(body, mesh=mesh, in_specs=in_specs, out_specs=out_specs, check_vma=False)
```
